1024 devices in a mesh: ctx: 256 (over x_hi, z, y), panel: 4 (over x_lo, core).
Axes of the slice: x: 4 (x_hi: 2, x_lo: 2; x = x_hi * 2 + x_lo), y: 4, z: 32, core: 2. Of those that a mesh axis runs over, the one named last changes fastest.
Arguments:
- se_streams: bfloat16 [3, 36864, 4096], P(None, 'ctx', 'panel'), may hold values from -6 to 6
- se_short: float32 [3, 3, 4096], P(None, None, 'panel'), may hold values from -2 to 2
- se_filter: float32 [7, 4096], P(None, 'panel'), may hold values from -2 to 2
- medium_projected_streams: bfloat16 [3, 36864, 4096], P(None, 'ctx', 'panel'), may hold values from -6 to 6
- mr_short: float32 [3, 3, 4096], P(None, None, 'panel'), may hold values from -2 to 2
- medium_filter_raw: float32 [128, 4096], P(None, 'panel'), may hold values from -0.9 to 0.9
- mr_decay: float32 [4096], P('panel'), may hold values from 0.003 to 0.1
- queries: bfloat16 [36864, 4096], P('ctx', 'panel'), may hold values from -180 to 180
- keys: bfloat16 [36864, 4096], P('ctx', 'panel'), may hold values from -6 to 6
- values: bfloat16 [36864, 4096], P('ctx', 'panel'), may hold values from -6 to 6
Outputs:
- se_out: bfloat16 [36864, 4096], P('ctx', 'panel')
- mr_out: bfloat16 [36864, 4096], P('ctx', 'panel')
- attn_out: bfloat16 [36864, 4096], P('ctx', 'panel')
The draws below stay inside these ranges and needn't reach their ends.
All inputs are finite; a program needn't handle non-finite values.
Results may differ from the reference program's by a relative error of at most 0.008.
Values may be sent and summed in bfloat16 or wider, within the bound.
A program may use at most 32 MiB of HBM per device.

```python
import math
import jax
import jax.numpy as jnp
from jax import lax

CHANNEL_SHARD = 4096
HD = 128
TOKENS_PER_SHARD = 144
FEATURIZER_TAPS = 3
LSE = 7
MEDIUM_TAPS = 128
S = 36864
N_CTX = 256


def pair_draw(key):
    base = jax.random.fold_in(key, 11)
    key_q, key_k = jax.random.split(base)
    query_all = jax.random.truncated_normal(key_q, -6.0, 6.0, (S, CHANNEL_SHARD), jnp.float32)
    key_all = jax.random.truncated_normal(key_k, -6.0, 6.0, (S, CHANNEL_SHARD), jnp.float32)
    return (query_all, key_all)


def draw_queries(key, part):
    return pair_draw(key)[0].astype(jnp.bfloat16)


def draw_keys(key, part):
    return pair_draw(key)[1].astype(jnp.bfloat16)


def level_of(own_key, extent, pieces, low, high):
    loudness = 1.0
    for axis_at, shards_of in pieces:
        heights = jax.random.uniform(jax.random.fold_in(jax.random.fold_in(own_key, 6), axis_at), (shards_of,), jnp.float32, low / len(pieces), high / len(pieces))
        loudness = loudness * jnp.repeat(jnp.exp(heights), extent[axis_at] // shards_of).reshape((-1,) + (1,) * (len(extent) - 1 - axis_at))
    return loudness


def gaussian(own_key, dims, scale, reach, pieces=(), kind=jnp.bfloat16):
    array = scale * jax.random.normal(own_key, dims, jnp.float32)
    if pieces:
        array = array * level_of(own_key, dims, pieces, -0.22, 0.18)
    return jnp.clip(array, -reach, reach).astype(kind)


def setup_inputs(seed: int = 0) -> dict:
    key_list = jax.random.split(jax.random.key(seed), 11)
    se_streams = gaussian(key_list[0], (3, S, CHANNEL_SHARD), 1.0, 6.0, ((1, 256), (2, 4)))
    se_short = gaussian(key_list[1], (3, FEATURIZER_TAPS, CHANNEL_SHARD), 0.4, 2.0, ((2, 4),), jnp.float32)
    se_filter = gaussian(key_list[2], (LSE, CHANNEL_SHARD), 0.4, 2.0, ((1, 4),), jnp.float32)
    medium_projected_streams = gaussian(key_list[3], (3, S, CHANNEL_SHARD), 1.0, 6.0, ((1, 256), (2, 4)))
    mr_short = gaussian(key_list[4], (3, FEATURIZER_TAPS, CHANNEL_SHARD), 0.4, 2.0, ((2, 4),), jnp.float32)
    medium_filter_raw = gaussian(key_list[5], (MEDIUM_TAPS, CHANNEL_SHARD), 0.15, 0.9, ((1, 4),), jnp.float32)
    mr_decay = jnp.clip(jnp.exp(math.log(0.1) - 3.506558 * jax.random.uniform(key_list[6], (CHANNEL_SHARD,), jnp.float32) ** level_of(key_list[6], (CHANNEL_SHARD,), ((0, 4),), -0.2, 0.2)), 0.003, 0.1)
    queries = draw_queries(jax.random.fold_in(key_list[10], 71), 0)
    keys = draw_keys(jax.random.fold_in(key_list[10], 71), 0)
    values = gaussian(key_list[9], (S, CHANNEL_SHARD), 1.0, 6.0, ((0, 256), (1, 4)))
    return {"se_streams": se_streams, "se_short": se_short, "se_filter": se_filter, "medium_projected_streams": medium_projected_streams, "mr_short": mr_short, "medium_filter_raw": medium_filter_raw, "mr_decay": mr_decay, "queries": queries, "keys": keys, "values": values}


def featurize(ext, short):
    taps = short.shape[1]
    count = ext.shape[1]
    total = short[:, 0][:, None, :] * ext[:, taps - 1:count, :].astype(jnp.float32)
    for j in range(1, taps):
        total = total + short[:, j][:, None, :] * ext[:, taps - 1 - j:count - j, :].astype(jnp.float32)
    return total

def long_conv(product, filt):
    taps = filt.shape[0]
    count = product.shape[0]
    pf = product.astype(jnp.float32)
    total = filt[0][None, :] * pf[taps - 1:count]
    for j in range(1, taps):
        total = total + filt[j][None, :] * pf[taps - 1 - j:count - j]
    return total

def hyena_full(streams, short, filt):
    width = math.gcd(CHANNEL_SHARD, 256)
    nblk = CHANNEL_SHARD // width
    taps = filt.shape[0]
    blocks = streams.reshape(3, S, nblk, width).transpose(2, 0, 1, 3)
    shorts = short.reshape(3, FEATURIZER_TAPS, nblk, width).transpose(2, 0, 1, 3)
    filts = filt.reshape(taps, nblk, width).transpose(1, 0, 2)

    def one(args):
        block, sblk, fblk = args
        ext = jnp.concatenate([jnp.zeros((3, FEATURIZER_TAPS - 1, width), block.dtype), block], axis=1)
        feats = featurize(ext, sblk)
        product = (feats[1] * feats[2]).astype(jnp.bfloat16)
        padded = jnp.concatenate([jnp.zeros((taps - 1, width), jnp.bfloat16), product], axis=0)
        return feats[0] * long_conv(padded, fblk)
    out = lax.map(one, (blocks, shorts, filts))
    return out.transpose(1, 0, 2).reshape(S, CHANNEL_SHARD)

def normalize(mixed):
    scale = lax.rsqrt(lax.optimization_barrier(jnp.mean(mixed * mixed, axis=-1)) + 1e-06)
    return (mixed * scale[:, None]).astype(jnp.bfloat16)

def attend(qblk, kblk, value_block, qpos, kpos):
    heads = qblk.shape[1] // HD
    q3 = qblk.reshape(-1, heads, HD)
    k3 = kblk.reshape(-1, heads, HD)
    v3 = value_block.reshape(-1, heads, HD)
    scores = jnp.einsum('qhd,khd->hqk', q3.astype(jnp.float32), k3.astype(jnp.float32)) * (1.0 / math.sqrt(HD))
    valid = (kpos[None, :] >= 0) & (kpos[None, :] <= qpos[:, None])
    masked = jnp.where(valid[None], scores, -1e+30)
    top = lax.optimization_barrier(jnp.max(masked, axis=-1, keepdims=True))
    raw = jnp.exp(masked - top)
    total = lax.optimization_barrier(jnp.sum(raw, axis=-1))
    probs = raw.astype(jnp.bfloat16)
    out = jnp.einsum('hqk,khd->qhd', probs.astype(jnp.float32), v3.astype(jnp.float32))
    out = out / total.T[:, :, None]
    return out.reshape(qblk.shape[0], -1)

def reference(se_streams, se_short, se_filter, medium_projected_streams, mr_short, medium_filter_raw, mr_decay, queries, keys, values):
    step_index = jnp.arange(MEDIUM_TAPS, dtype=jnp.float32)
    mr_taps = medium_filter_raw * jnp.exp(-mr_decay[None, :] * step_index[:, None])
    se_out = normalize(hyena_full(se_streams, se_short, se_filter))
    mr_out = normalize(hyena_full(medium_projected_streams, mr_short, mr_taps))
    zeroed_rows = jnp.zeros((TOKENS_PER_SHARD, CHANNEL_SHARD), jnp.bfloat16)
    kpad = jnp.concatenate([zeroed_rows, keys], axis=0)
    value_padded = jnp.concatenate([zeroed_rows, values], axis=0)
    local = jnp.arange(TOKENS_PER_SHARD, dtype=jnp.int32)
    wide = jnp.arange(2 * TOKENS_PER_SHARD, dtype=jnp.int32)

    def block(index):
        start_offset = (index * TOKENS_PER_SHARD).astype(jnp.int32)
        qblk = lax.dynamic_slice_in_dim(queries, start_offset, TOKENS_PER_SHARD, 0)
        kblk = lax.dynamic_slice_in_dim(kpad, start_offset, 2 * TOKENS_PER_SHARD, 0)
        value_block = lax.dynamic_slice_in_dim(value_padded, start_offset, 2 * TOKENS_PER_SHARD, 0)
        return attend(qblk, kblk, value_block, start_offset + local, start_offset - TOKENS_PER_SHARD + wide)
    mixed = lax.map(block, jnp.arange(N_CTX, dtype=jnp.int32)).reshape(S, CHANNEL_SHARD)
    return (se_out, mr_out, normalize(mixed))
```

```python
import functools
import math

import jax
import jax.numpy as jnp
from jax import lax
from jax.experimental import pallas as pl
from jax.experimental.pallas import tpu as pltpu
from jax.sharding import PartitionSpec as P

CHANNELS = 4096
HD = 128
T = 144
TAPS = 128
LSE = 7
HEADS = 8
WIDTH = HEADS * HD
F32 = jnp.float32
BF16 = jnp.bfloat16
MESH = pl.DeviceIdType.MESH
HIGHEST = lax.Precision.HIGHEST


def rows(t, count):
    return pl.ds(pl.multiple_of(t * 8, 8), count * 8)


def to_time(src, dst, start):
    def step(i, carry):
        r = pl.multiple_of(i * 16, 16)
        x = src[pl.ds(r, 16), :].astype(F32)
        for half in range(2):
            for k in range(8):
                dst[pl.ds((start + r + half * 8) * 8 + k, 8, stride=8), :] = x[
                    half * 8 : half * 8 + 8, k * HD : (k + 1) * HD
                ]
        return carry

    lax.fori_loop(0, T // 16, step, 0)


def spread(value, count):
    return jnp.concatenate([value] * count, axis=0)


def feature(u, w, base, t, count):
    total = spread(w[rows(base, 1), :], count) * u[rows(t + 2, count), :]
    for j in range(1, 3):
        total = total + spread(w[rows(base + j, 1), :], count) * u[rows(t + 2 - j, count), :]
    return total


def kernel(
    n_ctx, n_panel,
    se_u, se_w, se_f, mr_u, mr_w, mr_raw, decay, q, k, v,
    se_out, mr_out, at_out,
    ub, wb, fb, rawb, decb, qb, kcat, vcat,
    ut, wt, ft, taps, se_p, mr_p, se_mix, mr_mix, at_mix, bias, sq,
    rim_out, rim_in, p_out, p_in, st_out, st_in,
    load_sem, rim_sem, p_sem, k_send, k_recv, v_send, v_recv,
    st_send, st_recv,
):
    c = lax.axis_index("ctx")
    p = lax.axis_index("panel")
    is_first = c == 0
    has_dst = c < n_ctx - 1
    dst = (lax.rem(c + 1, n_ctx), p)
    src = (lax.rem(c + n_ctx - 1, n_ctx), p)

    loads = []

    def load(source, target):
        copy = pltpu.make_async_copy(source, target, load_sem.at[len(loads)])
        copy.start()
        loads.append(copy)
        return copy

    l_mr = [load(mr_u.at[i], ub.at[3 + i]) for i in (1, 2)]
    l_mw = load(mr_w, wb.at[1])
    l_sw = load(se_w, wb.at[0])
    l_se = [load(se_u.at[i], ub.at[i]) for i in (1, 2)]
    l_m0 = load(mr_u.at[0], ub.at[3])
    l_s0 = load(se_u.at[0], ub.at[0])
    l_f = load(se_f, fb)
    l_raw = load(mr_raw, rawb)
    l_dec = load(decay, decb)
    l_q = load(q, qb)
    l_k = load(k, kcat.at[pl.ds(T, T), :])
    l_v = load(v, vcat.at[pl.ds(T, T), :])

    barrier = pltpu.get_barrier_semaphore()

    @pl.when(jnp.logical_not(is_first))
    def _():
        pl.semaphore_signal(barrier, inc=1, device_id=src, device_id_type=MESH)

    for r in range(1, n_panel):
        pl.semaphore_signal(
            barrier, inc=1, device_id=(c, lax.rem(p + r, n_panel)), device_id_type=MESH
        )

    l_mw.wait()
    l_sw.wait()
    for b in range(2):
        for i in range(3):
            for j in range(3):
                for kk in range(8):
                    wt[pl.ds((b * 9 + i * 3 + j) * 8 + kk, 1), :] = wb[
                        b, i, pl.ds(j, 1), kk * HD : (kk + 1) * HD
                    ]
    zero_halo = jnp.zeros((16, HD), F32)
    for i in range(6):
        ut[i, pl.ds(0, 16), :] = zero_halo

    def products(block, out, shift, t, count):
        first = feature(ut.at[block * 3 + 1], wt, block * 9 + 3, t, count)
        second = feature(ut.at[block * 3 + 2], wt, block * 9 + 6, t, count)
        rounded = (first * second).astype(BF16)
        out[rows(t + shift, count), :] = rounded.astype(F32)
        return rounded

    for copy in l_mr:
        copy.wait()
    for i in (4, 5):
        to_time(ub.at[i], ut.at[i], 2)

    def mr_low(i, carry):
        products(1, mr_p, TAPS, i * 8, 8)
        return carry

    def mr_high(i, carry):
        t = i * 8
        rounded = products(1, mr_p, TAPS, t, 8)
        p_out[rows(t - 16, 8), :] = rounded
        return carry

    lax.fori_loop(0, 2, mr_low, 0)
    lax.fori_loop(2, 18, mr_high, 0)

    for copy in l_se:
        copy.wait()
    for i in (1, 2):
        to_time(ub.at[i], ut.at[i], 2)

    def se_low(i, carry):
        products(0, se_p, 8, i * 8, 8)
        return carry

    lax.fori_loop(0, 17, se_low, 0)
    rim_out[pl.ds(0, 64), :] = products(0, se_p, 8, 136, 8)
    l_m0.wait()
    l_s0.wait()
    for i in (3, 0):
        to_time(ub.at[i], ut.at[i], 2)
    for i in range(6):
        rim_out[pl.ds(64 + i * 16, 16), :] = ut[i, pl.ds(T * 8, 16), :].astype(BF16)

    pl.semaphore_wait(barrier, (n_panel - 1) + has_dst.astype(jnp.int32))

    def head(h):
        return pl.ds(pl.multiple_of(h * HD, HD), HD)

    rim_copy = pltpu.make_async_remote_copy(
        rim_out, rim_in, rim_sem.at[0], rim_sem.at[1], device_id=dst, device_id_type=MESH
    )
    p_copy = pltpu.make_async_remote_copy(
        p_out, p_in, p_sem.at[0], p_sem.at[1], device_id=dst, device_id_type=MESH
    )

    def k_copy(h):
        return pltpu.make_async_remote_copy(
            k.at[:, head(h)], kcat.at[pl.ds(0, T), head(h)], k_send.at[h], k_recv.at[h],
            device_id=dst, device_id_type=MESH,
        )

    def v_copy(h):
        return pltpu.make_async_remote_copy(
            v.at[:, head(h)], vcat.at[pl.ds(0, T), head(h)], v_send.at[h], v_recv.at[h],
            device_id=dst, device_id_type=MESH,
        )

    @pl.when(has_dst)
    def _():
        rim_copy.start()
        p_copy.start()

        def send(h, carry):
            k_copy(h).start()
            v_copy(h).start()
            return carry

        lax.fori_loop(0, HEADS, send, 0)

    l_f.wait()
    for j in range(LSE):
        for kk in range(8):
            ft[pl.ds(j * 8 + kk, 1), :] = fb[pl.ds(j, 1), kk * HD : (kk + 1) * HD]
    l_raw.wait()
    l_dec.wait()

    def tap_rows(i, carry):
        r = pl.multiple_of(i * 8, 8)
        x = rawb[pl.ds(r, 8), :]
        for kk in range(8):
            taps[pl.ds(r * 8 + kk, 8, stride=8), :] = x[:, kk * HD : (kk + 1) * HD]
        return carry

    lax.fori_loop(0, TAPS // 8, tap_rows, 0)

    def tap_decay(j, carry):
        jf = j.astype(F32)
        taps[rows(j, 1), :] = taps[rows(j, 1), :] * jnp.exp(-decb[...] * jf)
        return carry

    lax.fori_loop(0, TAPS, tap_decay, 0)

    queries_at = lax.broadcasted_iota(jnp.int32, (T, 2 * T), 0)
    keys_at = lax.broadcasted_iota(jnp.int32, (T, 2 * T), 1)
    low = lax.select(is_first, T, 0)
    seen = jnp.logical_and(keys_at <= queries_at + T, keys_at >= low)
    bias[...] = jnp.where(seen, 0.0, -1e30)

    def when_fed(value):
        pl.when(jnp.logical_not(is_first))(value)

    @pl.when(is_first)
    def _():
        rim_in[...] = jnp.zeros((160, HD), BF16)
        p_in[...] = jnp.zeros((TAPS * 8, HD), BF16)
        kcat[pl.ds(0, T), :] = jnp.zeros((T, WIDTH), BF16)
        vcat[pl.ds(0, T), :] = jnp.zeros((T, WIDTH), BF16)

    when_fed(rim_copy.wait_recv)
    for i in range(6):
        ut[i, pl.ds(0, 16), :] = rim_in[pl.ds(64 + i * 16, 16), :].astype(F32)
    se_p[pl.ds(0, 64), :] = rim_in[pl.ds(0, 64), :].astype(F32)
    products(0, se_p, 8, 0, 2)
    products(1, mr_p, TAPS, 0, 2)

    def se_block(i, carry):
        t = i * 8
        total = spread(ft[pl.ds(0, 8), :], 8) * se_p[rows(t + 8, 8), :]
        for j in range(1, LSE):
            total = total + spread(ft[pl.ds(j * 8, 8), :], 8) * se_p[rows(t + 8 - j, 8), :]
        se_mix[rows(t, 8), :] = total * feature(ut.at[0], wt, 0, t, 8)
        return carry

    lax.fori_loop(0, T // 8, se_block, 0)

    when_fed(p_copy.wait_recv)

    def prev_p(i, carry):
        mr_p[rows(i * 8, 8), :] = p_in[rows(i * 8, 8), :].astype(F32)
        return carry

    lax.fori_loop(0, TAPS // 8, prev_p, 0)

    block = 16

    def mr_block(i, carry):
        t = i * block

        def tap_group(g, acc):
            j0 = g * 8
            acc = list(acc)
            window = [mr_p[rows(TAPS + t - j0 - 7 + s, 1), :] for s in range(block + 7)]
            for jj in range(8):
                tap = taps[rows(j0 + jj, 1), :]
                for s in range(block):
                    acc[s] = acc[s] + tap * window[s + 7 - jj]
            return tuple(acc)

        zero = jnp.zeros((8, HD), F32)
        acc = lax.fori_loop(0, TAPS // 8, tap_group, (zero,) * block)
        gate = feature(ut.at[3], wt, 9, t, block)
        for s in range(block):
            mr_mix[rows(t + s, 1), :] = acc[s] * gate[s * 8 : s * 8 + 8]
        return carry

    lax.fori_loop(0, T // block, mr_block, 0)

    def squares(mix, out_index):
        def step(i, carry):
            base = pl.multiple_of(i * 64, 64)
            total = jnp.zeros((8, HD), F32)
            for kk in range(8):
                x = mix[pl.ds(base + kk, 8, stride=8), :]
                total = total + x * x
            sq[out_index, pl.ds(pl.multiple_of(i * 8, 8), 8), :] = total
            return carry

        lax.fori_loop(0, T // 8, step, 0)

    ones = jnp.ones((8, HD), F32)

    def row_sums(index):
        return lax.dot_general(
            ones, sq[index], (((1,), (1,)), ((), ())),
            precision=HIGHEST, preferred_element_type=F32,
        )

    def st_copy(s, r):
        return pltpu.make_async_remote_copy(
            st_out.at[s], st_in.at[s, r - 1], st_send.at[s, r - 1], st_recv.at[s, r - 1],
            device_id=(c, lax.rem(p + r, n_panel)), device_id_type=MESH,
        )

    def share(s):
        for r in range(1, n_panel):
            st_copy(s, r).start()

    pick = (lax.broadcasted_iota(jnp.int32, (8, HD), 0) == 0).astype(F32)

    def scales(s, index):
        total = st_out[s, index, :, :T]
        for r in range(1, n_panel):
            total = total + st_in[s, r - 1, index, :, :T]
        scale = lax.rsqrt(total / CHANNELS + 1e-06)
        return lax.dot_general(
            scale, pick, (((0,), (0,)), ((), ())),
            precision=HIGHEST, preferred_element_type=F32,
        )

    squares(se_mix, 0)
    squares(mr_mix, 1)
    st_out[0, 0, :, :T] = row_sums(0)
    st_out[0, 1, :, :T] = row_sums(1)
    share(0)

    l_q.wait()
    l_k.wait()
    l_v.wait()
    sq[2] = jnp.zeros((T, HD), F32)

    def attend(h, carry):
        when_fed(k_copy(h).wait_recv)
        scores = lax.dot_general(
            qb[:, head(h)], kcat[:, head(h)], (((1,), (1,)), ((), ())),
            preferred_element_type=F32,
        )
        scores = scores * (1.0 / math.sqrt(HD)) + bias[...]
        top = jnp.max(scores, axis=1, keepdims=True)
        raw = jnp.exp(scores - top)
        total = jnp.sum(raw, axis=1, keepdims=True)
        when_fed(v_copy(h).wait_recv)
        mixed = lax.dot_general(
            raw.astype(BF16), vcat[:, head(h)], (((1,), (0,)), ((), ())),
            preferred_element_type=F32,
        )
        mixed = mixed * (1.0 / total)
        at_mix[:, head(h)] = mixed
        sq[2] = sq[2] + mixed * mixed
        return carry

    lax.fori_loop(0, HEADS - 2, attend, 0)

    for r in range(1, n_panel):
        st_copy(0, r).wait_recv()
    for index, mix, out in ((0, se_mix, se_out), (1, mr_mix, mr_out)):
        sq[index] = scales(0, index)

        def finish(i, carry):
            r = pl.multiple_of(i * 16, 16)
            for kk in range(8):
                parts = []
                for hh in range(2):
                    x = mix[pl.ds((r + hh * 8) * 8 + kk, 8, stride=8), :]
                    parts.append(x * sq[index, pl.ds(r + hh * 8, 8), :])
                out[pl.ds(r, 16), kk * HD : (kk + 1) * HD] = jnp.concatenate(parts, 0).astype(BF16)
            return carry

        lax.fori_loop(0, T // 16, finish, 0)

    lax.fori_loop(HEADS - 2, HEADS, attend, 0)

    st_out[1, 0, :, :T] = row_sums(2)
    share(1)
    for r in range(1, n_panel):
        st_copy(1, r).wait_recv()
    sq[2] = scales(1, 0)
    for h in range(HEADS):
        at_out[:, h * HD : (h + 1) * HD] = (at_mix[:, h * HD : (h + 1) * HD] * sq[2]).astype(BF16)

    for s in range(2):
        for r in range(1, n_panel):
            st_copy(s, r).wait_send()

    @pl.when(has_dst)
    def _():
        rim_copy.wait_send()
        p_copy.wait_send()

        def sent(h, carry):
            k_copy(h).wait_send()
            v_copy(h).wait_send()
            return carry

        lax.fori_loop(0, HEADS, sent, 0)


def body(n_ctx, n_panel, se_u, se_w, se_f, mr_u, mr_w, mr_raw, mr_decay, q, k, v):
    anywhere = pl.BlockSpec(memory_space=pl.ANY)
    vmem = pl.BlockSpec(memory_space=pltpu.VMEM)
    out = jax.ShapeDtypeStruct((T, WIDTH), BF16)
    dma = pltpu.SemaphoreType.DMA
    return pl.pallas_call(
        functools.partial(kernel, n_ctx, n_panel),
        out_shape=(out, out, out),
        in_specs=[anywhere] * 10,
        out_specs=(vmem, vmem, vmem),
        scratch_shapes=[
            pltpu.VMEM((6, T, WIDTH), BF16),
            pltpu.VMEM((2, 3, 3, WIDTH), F32),
            pltpu.VMEM((LSE, WIDTH), F32),
            pltpu.VMEM((TAPS, WIDTH), F32),
            pltpu.VMEM((8, HD), F32),
            pltpu.VMEM((T, WIDTH), BF16),
            pltpu.VMEM((2 * T, WIDTH), BF16),
            pltpu.VMEM((2 * T, WIDTH), BF16),
            pltpu.VMEM((6, (T + 2) * 8, HD), F32),
            pltpu.VMEM((18 * 8, HD), F32),
            pltpu.VMEM((8 * 8, HD), F32),
            pltpu.VMEM((TAPS * 8, HD), F32),
            pltpu.VMEM(((T + 8) * 8, HD), F32),
            pltpu.VMEM(((T + TAPS) * 8, HD), F32),
            pltpu.VMEM((T * 8, HD), F32),
            pltpu.VMEM((T * 8, HD), F32),
            pltpu.VMEM((T, WIDTH), F32),
            pltpu.VMEM((T, 2 * T), F32),
            pltpu.VMEM((3, T, HD), F32),
            pltpu.VMEM((160, HD), BF16),
            pltpu.VMEM((160, HD), BF16),
            pltpu.VMEM((TAPS * 8, HD), BF16),
            pltpu.VMEM((TAPS * 8, HD), BF16),
            pltpu.VMEM((2, 2, 8, 256), F32),
            pltpu.VMEM((2, n_panel - 1, 2, 8, 256), F32),
            dma((14,)),
            dma((2,)),
            dma((2,)),
            dma((HEADS,)),
            dma((HEADS,)),
            dma((HEADS,)),
            dma((HEADS,)),
            dma((2, n_panel - 1)),
            dma((2, n_panel - 1)),
        ],
        compiler_params=pltpu.CompilerParams(collective_id=0, has_side_effects=True),
        name="mixer",
    )(se_u, se_w, se_f, mr_u, mr_w, mr_raw, mr_decay.reshape(8, HD), q, k, v)


def solution(mesh):
    placed = (
        P(None, "ctx", "panel"),
        P(None, None, "panel"),
        P(None, "panel"),
        P(None, "ctx", "panel"),
        P(None, None, "panel"),
        P(None, "panel"),
        P("panel"),
        P("ctx", "panel"),
        P("ctx", "panel"),
        P("ctx", "panel"),
    )
    return jax.shard_map(
        functools.partial(body, mesh.shape["ctx"], mesh.shape["panel"]),
        mesh=mesh,
        in_specs=placed,
        out_specs=(P("ctx", "panel"), P("ctx", "panel"), P("ctx", "panel")),
        check_vma=False,
    )
```

```python
import functools
import math

import jax
import jax.numpy as jnp
from jax import lax
from jax.experimental import pallas as pl
from jax.experimental.pallas import tpu as pltpu
from jax.sharding import PartitionSpec as P

CHANNELS = 4096
HD = 128
T = 144
TAPS = 128
LSE = 7
HEADS = 8
PAIRS = HEADS // 2
QUARTERS = 4
PART_P = TAPS * 8 // QUARTERS
WIDTH = HEADS * HD
F32 = jnp.float32
BF16 = jnp.bfloat16
MESH = pl.DeviceIdType.MESH
HIGHEST = lax.Precision.HIGHEST


def rows(t, count):
    return pl.ds(pl.multiple_of(t * 8, 8), count * 8)


def to_time(src, dst, start):
    def step(i, carry):
        r = pl.multiple_of(i * 16, 16)
        x = src[pl.ds(r, 16), :].astype(F32)
        for half in range(2):
            for k in range(8):
                dst[pl.ds((start + r + half * 8) * 8 + k, 8, stride=8), :] = x[
                    half * 8 : half * 8 + 8, k * HD : (k + 1) * HD
                ]
        return carry

    lax.fori_loop(0, T // 16, step, 0)


def spread(value, count):
    return jnp.concatenate([value] * count, axis=0)


def feature(u, w, base, t, count):
    total = spread(w[rows(base, 1), :], count) * u[rows(t + 2, count), :]
    for j in range(1, 3):
        total = total + spread(w[rows(base + j, 1), :], count) * u[rows(t + 2 - j, count), :]
    return total


def kernel(
    n_ctx, n_panel,
    se_u, se_w, se_f, mr_u, mr_w, mr_raw, decay, q, k, v,
    se_out, mr_out, at_out,
    ub, wb, fb, rawb, decb, qb, kcat, vcat,
    ut, wt, ft, taps, se_p, mr_p, se_mix, mr_mix, at_mix, bias, sq,
    rim_out, rim_in, p_out, p_in, st_out, st_in,
    load_sem, rim_sem, p_send, p_recv, k_send, k_recv, v_send, v_recv, st_send, st_recv,
):
    c = lax.axis_index("ctx")
    p = lax.axis_index("panel")
    is_first = c == 0
    has_dst = c < n_ctx - 1
    dst = (lax.rem(c + 1, n_ctx), p)
    src = (lax.rem(c + n_ctx - 1, n_ctx), p)

    loads = []

    def load(source, target):
        copy = pltpu.make_async_copy(source, target, load_sem.at[len(loads)])
        copy.start()
        loads.append(copy)
        return copy

    l_kv = []
    for h in range(HEADS):
        lanes = pl.ds(h * HD, HD)
        l_kv.append(load(k.at[:, lanes], kcat.at[h, pl.ds(T, T), :]))
        l_kv.append(load(v.at[:, lanes], vcat.at[h, pl.ds(T, T), :]))
    l_mr = [load(mr_u.at[i], ub.at[3 + i]) for i in (1, 2)]
    l_mw = load(mr_w, wb.at[1])
    l_sw = load(se_w, wb.at[0])
    l_se = [load(se_u.at[i], ub.at[i]) for i in (1, 2)]
    l_m0 = load(mr_u.at[0], ub.at[3])
    l_s0 = load(se_u.at[0], ub.at[0])
    l_f = load(se_f, fb)
    l_raw = load(mr_raw, rawb)
    l_dec = load(decay, decb)
    l_q = load(q, qb)

    barrier = pltpu.get_barrier_semaphore()

    @pl.when(jnp.logical_not(is_first))
    def _():
        pl.semaphore_signal(barrier, inc=1, device_id=src, device_id_type=MESH)

    for r in range(1, n_panel):
        pl.semaphore_signal(
            barrier, inc=1, device_id=(c, lax.rem(p + r, n_panel)), device_id_type=MESH
        )

    l_mw.wait()
    l_sw.wait()
    for b in range(2):
        for i in range(3):
            for j in range(3):
                for kk in range(8):
                    wt[pl.ds((b * 9 + i * 3 + j) * 8 + kk, 1), :] = wb[
                        b, i, pl.ds(j, 1), kk * HD : (kk + 1) * HD
                    ]
    zero_halo = jnp.zeros((16, HD), F32)
    for i in range(6):
        ut[i, pl.ds(0, 16), :] = zero_halo

    def own(ref, pair):
        return ref.at[pl.ds(pair * 2, 2), pl.ds(T, T), :]

    def prior(ref, pair):
        return ref.at[pl.ds(pair * 2, 2), pl.ds(0, T), :]

    def remote(source, target, send, recv, device):
        return pltpu.make_async_remote_copy(
            source, target, send, recv, device_id=device, device_id_type=MESH
        )

    rim_copy = remote(rim_out, rim_in, rim_sem.at[0], rim_sem.at[1], dst)

    def p_part(ref, part):
        return ref.at[pl.ds(part * PART_P, PART_P), :]

    def p_copy(part):
        return remote(p_part(p_out, part), p_part(p_in, part), p_send.at[part], p_recv.at[part], dst)

    def k_copy(pair):
        target = prior(kcat, pair)
        return remote(own(kcat, pair), target, k_send.at[pair], k_recv.at[pair], dst)

    def v_copy(pair):
        target = prior(vcat, pair)
        return remote(own(vcat, pair), target, v_send.at[pair], v_recv.at[pair], dst)

    for copy in l_kv:
        copy.wait()
    pl.semaphore_wait(barrier, (n_panel - 1) + has_dst.astype(jnp.int32))

    @pl.when(has_dst)
    def _():
        k_copy(0).start()
        v_copy(0).start()

    def products(block, out, shift, t, count):
        first = feature(ut.at[block * 3 + 1], wt, block * 9 + 3, t, count)
        second = feature(ut.at[block * 3 + 2], wt, block * 9 + 6, t, count)
        rounded = (first * second).astype(BF16)
        out[rows(t + shift, count), :] = rounded.astype(F32)
        return rounded

    for copy in l_mr:
        copy.wait()
    for i in (4, 5):
        to_time(ub.at[i], ut.at[i], 2)

    def mr_low(i, carry):
        products(1, mr_p, TAPS, i * 8, 8)
        return carry

    def mr_high(i, carry):
        t = i * 8
        rounded = products(1, mr_p, TAPS, t, 8)
        p_out[rows(t - 16, 8), :] = rounded
        return carry

    lax.fori_loop(0, 2, mr_low, 0)
    lax.fori_loop(2, 18, mr_high, 0)

    for copy in l_se:
        copy.wait()
    for i in (1, 2):
        to_time(ub.at[i], ut.at[i], 2)

    @pl.when(has_dst)
    def _():
        for part in range(QUARTERS):
            p_copy(part).start()

    def se_low(i, carry):
        products(0, se_p, 8, i * 8, 8)
        return carry

    lax.fori_loop(0, 17, se_low, 0)
    rim_out[pl.ds(0, 64), :] = products(0, se_p, 8, 136, 8)
    l_m0.wait()
    l_s0.wait()
    for i in (3, 0):
        to_time(ub.at[i], ut.at[i], 2)
    for i in range(6):
        rim_out[pl.ds(64 + i * 16, 16), :] = ut[i, pl.ds(T * 8, 16), :].astype(BF16)

    @pl.when(has_dst)
    def _():
        rim_copy.start()
        for pair in range(1, PAIRS):
            k_copy(pair).start()
            v_copy(pair).start()

    def head(h):
        return pl.ds(pl.multiple_of(h * HD, HD), HD)

    l_f.wait()
    for j in range(LSE):
        for kk in range(8):
            ft[pl.ds(j * 8 + kk, 1), :] = fb[pl.ds(j, 1), kk * HD : (kk + 1) * HD]
    l_raw.wait()
    l_dec.wait()

    def tap_rows(i, carry):
        r = pl.multiple_of(i * 8, 8)
        x = rawb[pl.ds(r, 8), :]
        for kk in range(8):
            taps[pl.ds(r * 8 + kk, 8, stride=8), :] = x[:, kk * HD : (kk + 1) * HD]
        return carry

    lax.fori_loop(0, TAPS // 8, tap_rows, 0)

    def tap_decay(g, carry):
        for jj in range(8):
            j = g * 8 + jj
            taps[rows(j, 1), :] = taps[rows(j, 1), :] * jnp.exp(-decb[...] * j.astype(F32))
        return carry

    lax.fori_loop(0, TAPS // 8, tap_decay, 0)

    queries_at = lax.broadcasted_iota(jnp.int32, (T, 2 * T), 0)
    keys_at = lax.broadcasted_iota(jnp.int32, (T, 2 * T), 1)
    low = lax.select(is_first, T, 0)
    seen = jnp.logical_and(keys_at <= queries_at + T, keys_at >= low)
    bias[...] = jnp.where(seen, 0.0, -1e30)

    def when_fed(value):
        pl.when(jnp.logical_not(is_first))(value)

    @pl.when(is_first)
    def _():
        rim_in[...] = jnp.zeros((160, HD), BF16)
        p_in[...] = jnp.zeros((TAPS * 8, HD), BF16)
        for h in range(HEADS):
            kcat[h, pl.ds(0, T), :] = jnp.zeros((T, HD), BF16)
            vcat[h, pl.ds(0, T), :] = jnp.zeros((T, HD), BF16)


    def se_block(i, carry):
        t = i * 8
        total = spread(ft[pl.ds(0, 8), :], 8) * se_p[rows(t + 8, 8), :]
        for j in range(1, LSE):
            total = total + spread(ft[pl.ds(j * 8, 8), :], 8) * se_p[rows(t + 8 - j, 8), :]
        se_mix[rows(t, 8), :] = total * feature(ut.at[0], wt, 0, t, 8)
        return carry

    lax.fori_loop(1, T // 8, se_block, 0)


    block = 16

    def tap_group(t, g, acc):
        j0 = g * 8
        acc = list(acc)
        window = [mr_p[rows(TAPS + t - j0 - 7 + s, 1), :] for s in range(block + 7)]
        for jj in range(8):
            tap = taps[rows(j0 + jj, 1), :]
            for s in range(block):
                acc[s] = acc[s] + tap * window[s + 7 - jj]
        return tuple(acc)

    def mr_own(i, carry):
        t = i * block
        zero = jnp.zeros((8, HD), F32)
        acc = lax.fori_loop(0, i * 2 - 1, lambda g, acc: tap_group(t, g, acc), (zero,) * block)
        for s in range(block):
            mr_mix[rows(t + s, 1), :] = acc[s]
        return carry

    for s in range(block):
        mr_mix[rows(s, 1), :] = jnp.zeros((8, HD), F32)
    lax.fori_loop(1, T // block, mr_own, 0)

    l_q.wait()
    sq[2] = jnp.zeros((T, HD), F32)

    def squares(mix, out_index):
        def step(i, carry):
            base = pl.multiple_of(i * 64, 64)
            total = jnp.zeros((8, HD), F32)
            for kk in range(8):
                x = mix[pl.ds(base + kk, 8, stride=8), :]
                total = total + x * x
            sq[out_index, pl.ds(pl.multiple_of(i * 8, 8), 8), :] = total
            return carry

        lax.fori_loop(0, T // 8, step, 0)

    ones = jnp.ones((8, HD), F32)

    def row_sums(index):
        return lax.dot_general(
            ones, sq[index], (((1,), (1,)), ((), ())),
            precision=HIGHEST, preferred_element_type=F32,
        )

    def st_copy(s, r):
        return pltpu.make_async_remote_copy(
            st_out.at[s], st_in.at[s, r - 1], st_send.at[s, r - 1], st_recv.at[s, r - 1],
            device_id=(c, lax.rem(p + r, n_panel)), device_id_type=MESH,
        )

    def share(s):
        for r in range(1, n_panel):
            st_copy(s, r).start()

    pick = (lax.broadcasted_iota(jnp.int32, (8, HD), 0) == 0).astype(F32)

    def scales(s, index):
        total = st_out[s, index, :, :T]
        for r in range(1, n_panel):
            total = total + st_in[s, r - 1, index, :, :T]
        scale = lax.rsqrt(total / CHANNELS + 1e-06)
        return lax.dot_general(
            scale, pick, (((0,), (0,)), ((), ())),
            precision=HIGHEST, preferred_element_type=F32,
        )

    def attend(h, carry):
        scores = lax.dot_general(
            qb[:, head(h)], kcat[h], (((1,), (1,)), ((), ())),
            preferred_element_type=F32,
        )
        scores = scores * (1.0 / math.sqrt(HD)) + bias[...]
        top = jnp.max(scores, axis=1, keepdims=True)
        raw = jnp.exp(scores - top)
        total = jnp.sum(raw, axis=1, keepdims=True)
        mixed = lax.dot_general(
            raw.astype(BF16), vcat[h], (((1,), (0,)), ((), ())),
            preferred_element_type=F32,
        )
        mixed = mixed * (1.0 / total)
        at_mix[:, head(h)] = mixed
        sq[2] = sq[2] + mixed * mixed
        return carry

    def attend_pair(pair):
        when_fed(k_copy(pair).wait_recv)
        when_fed(v_copy(pair).wait_recv)
        lax.fori_loop(pair * 2, pair * 2 + 2, attend, 0)

    attend_pair(0)


    when_fed(rim_copy.wait_recv)
    for i in range(6):
        ut[i, pl.ds(0, 16), :] = rim_in[pl.ds(64 + i * 16, 16), :].astype(F32)
    se_p[pl.ds(0, 64), :] = rim_in[pl.ds(0, 64), :].astype(F32)
    products(0, se_p, 8, 0, 2)
    products(1, mr_p, TAPS, 0, 2)
    se_block(0, 0)
    for part in range(QUARTERS):
        when_fed(p_copy(part).wait_recv)

    def prev_p(i, carry):
        mr_p[rows(i * 8, 8), :] = p_in[rows(i * 8, 8), :].astype(F32)
        return carry

    lax.fori_loop(0, TAPS // 8, prev_p, 0)

    def mr_rest(i, carry):
        t = i * block
        acc = tuple(mr_mix[rows(t + s, 1), :] for s in range(block))
        start = lax.max(i * 2 - 1, 0)
        acc = lax.fori_loop(start, TAPS // 8, lambda g, acc: tap_group(t, g, acc), acc)
        gate = feature(ut.at[3], wt, 9, t, block)
        for s in range(block):
            mr_mix[rows(t + s, 1), :] = acc[s] * gate[s * 8 : s * 8 + 8]

        return carry

    lax.fori_loop(0, T // block, mr_rest, 0)

    attend_pair(1)

    squares(se_mix, 0)
    squares(mr_mix, 1)
    st_out[0, 0, :, :T] = row_sums(0)
    st_out[0, 1, :, :T] = row_sums(1)
    share(0)

    attend_pair(2)

    for r in range(1, n_panel):
        st_copy(0, r).wait_recv()
    for index, mix, out in ((0, se_mix, se_out), (1, mr_mix, mr_out)):
        sq[index] = scales(0, index)

        def finish(i, carry):
            r = pl.multiple_of(i * 16, 16)
            for kk in range(8):
                parts = []
                for hh in range(2):
                    x = mix[pl.ds((r + hh * 8) * 8 + kk, 8, stride=8), :]
                    parts.append(x * sq[index, pl.ds(r + hh * 8, 8), :])
                out[pl.ds(r, 16), kk * HD : (kk + 1) * HD] = jnp.concatenate(parts, 0).astype(BF16)
            return carry

        lax.fori_loop(0, T // 16, finish, 0)

    attend_pair(3)

    st_out[1, 0, :, :T] = row_sums(2)
    share(1)
    for r in range(1, n_panel):
        st_copy(1, r).wait_recv()
    sq[2] = scales(1, 0)
    for h in range(HEADS):
        at_out[:, h * HD : (h + 1) * HD] = (at_mix[:, h * HD : (h + 1) * HD] * sq[2]).astype(BF16)

    for s in range(2):
        for r in range(1, n_panel):
            st_copy(s, r).wait_send()

    @pl.when(has_dst)
    def _():
        rim_copy.wait_send()
        for part in range(QUARTERS):
            p_copy(part).wait_send()
        for pair in range(PAIRS):
            k_copy(pair).wait_send()
            v_copy(pair).wait_send()


def writer(a, b, c, x, y, z, sems):
    copies = [
        pltpu.make_async_copy(i, o, sems.at[n]) for n, (i, o) in enumerate(((a, x), (b, y), (c, z)))
    ]
    for copy in copies:
        copy.start()
    for copy in copies:
        copy.wait()


def body(n_ctx, n_panel, se_u, se_w, se_f, mr_u, mr_w, mr_raw, mr_decay, q, k, v):
    anywhere = pl.BlockSpec(memory_space=pl.ANY)
    vmem = pl.BlockSpec(memory_space=pltpu.VMEM)
    out = pltpu.VMEM((T, WIDTH), BF16)
    plain = jax.ShapeDtypeStruct((T, WIDTH), BF16)
    dma = pltpu.SemaphoreType.DMA
    mixed = pl.pallas_call(
        functools.partial(kernel, n_ctx, n_panel),
        out_shape=(out, out, out),
        in_specs=[anywhere] * 10,
        out_specs=(vmem, vmem, vmem),
        scratch_shapes=[
            pltpu.VMEM((6, T, WIDTH), BF16),
            pltpu.VMEM((2, 3, 3, WIDTH), F32),
            pltpu.VMEM((LSE, WIDTH), F32),
            pltpu.VMEM((TAPS, WIDTH), F32),
            pltpu.VMEM((8, HD), F32),
            pltpu.VMEM((T, WIDTH), BF16),
            pltpu.VMEM((HEADS, 2 * T, HD), BF16),
            pltpu.VMEM((HEADS, 2 * T, HD), BF16),
            pltpu.VMEM((6, (T + 2) * 8, HD), F32),
            pltpu.VMEM((18 * 8, HD), F32),
            pltpu.VMEM((8 * 8, HD), F32),
            pltpu.VMEM((TAPS * 8, HD), F32),
            pltpu.VMEM(((T + 8) * 8, HD), F32),
            pltpu.VMEM(((T + TAPS) * 8, HD), F32),
            pltpu.VMEM((T * 8, HD), F32),
            pltpu.VMEM((T * 8, HD), F32),
            pltpu.VMEM((T, WIDTH), F32),
            pltpu.VMEM((T, 2 * T), F32),
            pltpu.VMEM((3, T, HD), F32),
            pltpu.VMEM((160, HD), BF16),
            pltpu.VMEM((160, HD), BF16),
            pltpu.VMEM((TAPS * 8, HD), BF16),
            pltpu.VMEM((TAPS * 8, HD), BF16),
            pltpu.VMEM((2, 2, 8, 256), F32),
            pltpu.VMEM((2, n_panel - 1, 2, 8, 256), F32),
            dma((12 + 2 * HEADS,)),
            dma((2,)),
            dma((QUARTERS,)),
            dma((QUARTERS,)),
            dma((PAIRS,)),
            dma((PAIRS,)),
            dma((PAIRS,)),
            dma((PAIRS,)),
            dma((2, n_panel - 1)),
            dma((2, n_panel - 1)),
        ],
        compiler_params=pltpu.CompilerParams(collective_id=0, has_side_effects=True),
        name="mixer",
    )(se_u, se_w, se_f, mr_u, mr_w, mr_raw, mr_decay.reshape(8, HD), q, k, v)
    return pl.pallas_call(
        writer,
        out_shape=(plain, plain, plain),
        in_specs=[vmem] * 3,
        out_specs=[anywhere] * 3,
        scratch_shapes=[dma((3,))],
        name="writer",
    )(*(pltpu.with_memory_space_constraint(x, pltpu.VMEM) for x in mixed))


def solution(mesh):
    placed = (
        P(None, "ctx", "panel"),
        P(None, None, "panel"),
        P(None, "panel"),
        P(None, "ctx", "panel"),
        P(None, None, "panel"),
        P(None, "panel"),
        P("panel"),
        P("ctx", "panel"),
        P("ctx", "panel"),
        P("ctx", "panel"),
    )
    return jax.shard_map(
        functools.partial(body, mesh.shape["ctx"], mesh.shape["panel"]),
        mesh=mesh,
        in_specs=placed,
        out_specs=(P("ctx", "panel"), P("ctx", "panel"), P("ctx", "panel")),
        check_vma=False,
    )
```

```python
import functools
import math

import jax
import jax.numpy as jnp
from jax import lax
from jax.experimental import pallas as pl
from jax.experimental.pallas import tpu as pltpu
from jax.sharding import PartitionSpec as P

CHANNELS = 4096
HD = 128
T = 144
TAPS = 128
LSE = 7
HEADS = 8
PAIRS = HEADS // 2
QUARTERS = 4
PART_P = TAPS * 8 // QUARTERS
WIDTH = HEADS * HD
F32 = jnp.float32
BF16 = jnp.bfloat16
MESH = pl.DeviceIdType.MESH
HIGHEST = lax.Precision.HIGHEST


def rows(t, count):
    return pl.ds(pl.multiple_of(t * 8, 8), count * 8)


def to_time(src, dst, start):
    def step(i, carry):
        r = pl.multiple_of(i * 16, 16)
        x = src[pl.ds(r, 16), :].astype(F32)
        for half in range(2):
            for k in range(8):
                dst[pl.ds((start + r + half * 8) * 8 + k, 8, stride=8), :] = x[
                    half * 8 : half * 8 + 8, k * HD : (k + 1) * HD
                ]
        return carry

    lax.fori_loop(0, T // 16, step, 0)


def spread(value, count):
    return jnp.concatenate([value] * count, axis=0)


def feature(u, w, base, t, count):
    total = spread(w[rows(base, 1), :], count) * u[rows(t + 2, count), :]
    for j in range(1, 3):
        total = total + spread(w[rows(base + j, 1), :], count) * u[rows(t + 2 - j, count), :]
    return total


def kernel(
    n_ctx, n_panel,
    se_u, se_w, se_f, mr_u, mr_w, mr_raw, decay, q, k, v,
    se_out, mr_out, at_out,
    ub, wb, fb, rawb, decb, qb, kcat, vcat,
    ut, wt, ft, taps, se_p, mr_p, se_mix, mr_mix, at_mix, bias, sq,
    rim_out, rim_in, p_out, p_in, st_out, st_in,
    load_sem, rim_sem, p_send, p_recv, k_send, k_recv, v_send, v_recv, st_send, st_recv,
):
    c = lax.axis_index("ctx")
    p = lax.axis_index("panel")
    is_first = c == 0
    has_dst = c < n_ctx - 1
    dst = (lax.rem(c + 1, n_ctx), p)
    src = (lax.rem(c + n_ctx - 1, n_ctx), p)

    loads = []

    def load(source, target):
        copy = pltpu.make_async_copy(source, target, load_sem.at[len(loads)])
        copy.start()
        loads.append(copy)
        return copy

    l_kv = []
    for h in range(HEADS):
        lanes = pl.ds(h * HD, HD)
        l_kv.append(load(k.at[:, lanes], kcat.at[h, pl.ds(T, T), :]))
        l_kv.append(load(v.at[:, lanes], vcat.at[h, pl.ds(T, T), :]))
    l_mr = [load(mr_u.at[i], ub.at[3 + i]) for i in (1, 2)]
    l_mw = load(mr_w, wb.at[1])
    l_sw = load(se_w, wb.at[0])
    l_se = [load(se_u.at[i], ub.at[i]) for i in (1, 2)]
    l_m0 = load(mr_u.at[0], ub.at[3])
    l_s0 = load(se_u.at[0], ub.at[0])
    l_f = load(se_f, fb)
    l_raw = load(mr_raw, rawb)
    l_dec = load(decay, decb)
    l_q = load(q, qb)

    barrier = pltpu.get_barrier_semaphore()

    @pl.when(jnp.logical_not(is_first))
    def _():
        pl.semaphore_signal(barrier, inc=1, device_id=src, device_id_type=MESH)

    for r in range(1, n_panel):
        pl.semaphore_signal(
            barrier, inc=1, device_id=(c, lax.rem(p + r, n_panel)), device_id_type=MESH
        )

    def own(ref, pair):
        return ref.at[pl.ds(pair * 2, 2), pl.ds(T, T), :]

    def prior(ref, pair):
        return ref.at[pl.ds(pair * 2, 2), pl.ds(0, T), :]

    def remote(source, target, send, recv, device):
        return pltpu.make_async_remote_copy(
            source, target, send, recv, device_id=device, device_id_type=MESH
        )

    rim_copy = remote(rim_out, rim_in, rim_sem.at[0], rim_sem.at[1], dst)

    def p_part(ref, part):
        return ref.at[pl.ds(part * PART_P, PART_P), :]

    def p_copy(part):
        return remote(p_part(p_out, part), p_part(p_in, part), p_send.at[part], p_recv.at[part], dst)

    def k_copy(pair):
        target = prior(kcat, pair)
        return remote(own(kcat, pair), target, k_send.at[pair], k_recv.at[pair], dst)

    def v_copy(pair):
        target = prior(vcat, pair)
        return remote(own(vcat, pair), target, v_send.at[pair], v_recv.at[pair], dst)

    for copy in l_kv[:4]:
        copy.wait()
    pl.semaphore_wait(barrier, (n_panel - 1) + has_dst.astype(jnp.int32))

    @pl.when(has_dst)
    def _():
        k_copy(0).start()
        v_copy(0).start()

    l_mw.wait()
    l_sw.wait()
    for b in range(2):
        for i in range(3):
            for j in range(3):
                for kk in range(8):
                    wt[pl.ds((b * 9 + i * 3 + j) * 8 + kk, 1), :] = wb[
                        b, i, pl.ds(j, 1), kk * HD : (kk + 1) * HD
                    ]
    zero_halo = jnp.zeros((16, HD), F32)
    for i in range(6):
        ut[i, pl.ds(0, 16), :] = zero_halo

    def products(block, out, shift, t, count):
        first = feature(ut.at[block * 3 + 1], wt, block * 9 + 3, t, count)
        second = feature(ut.at[block * 3 + 2], wt, block * 9 + 6, t, count)
        rounded = (first * second).astype(BF16)
        out[rows(t + shift, count), :] = rounded.astype(F32)
        return rounded

    for copy in l_kv[4:] + l_mr:
        copy.wait()
    for i in (4, 5):
        to_time(ub.at[i], ut.at[i], 2)

    def mr_low(i, carry):
        products(1, mr_p, TAPS, i * 8, 8)
        return carry

    def mr_high(i, carry):
        t = i * 8
        rounded = products(1, mr_p, TAPS, t, 8)
        p_out[rows(t - 16, 8), :] = rounded
        return carry

    lax.fori_loop(0, 2, mr_low, 0)
    lax.fori_loop(2, 18, mr_high, 0)

    for copy in l_se:
        copy.wait()
    for i in (1, 2):
        to_time(ub.at[i], ut.at[i], 2)

    @pl.when(has_dst)
    def _():
        for part in range(QUARTERS):
            p_copy(part).start()

    def se_low(i, carry):
        products(0, se_p, 8, i * 8, 8)
        return carry

    lax.fori_loop(0, 17, se_low, 0)
    rim_out[pl.ds(0, 64), :] = products(0, se_p, 8, 136, 8)
    l_m0.wait()
    l_s0.wait()
    for i in (3, 0):
        to_time(ub.at[i], ut.at[i], 2)
    for i in range(6):
        rim_out[pl.ds(64 + i * 16, 16), :] = ut[i, pl.ds(T * 8, 16), :].astype(BF16)

    @pl.when(has_dst)
    def _():
        rim_copy.start()
        for pair in range(1, PAIRS):
            k_copy(pair).start()
            v_copy(pair).start()

    l_f.wait()
    for j in range(LSE):
        for kk in range(8):
            ft[pl.ds(j * 8 + kk, 1), :] = fb[pl.ds(j, 1), kk * HD : (kk + 1) * HD]
    l_raw.wait()
    l_dec.wait()

    def tap_rows(i, carry):
        r = pl.multiple_of(i * 8, 8)
        x = rawb[pl.ds(r, 8), :]
        for kk in range(8):
            taps[pl.ds(r * 8 + kk, 8, stride=8), :] = x[:, kk * HD : (kk + 1) * HD]
        return carry

    lax.fori_loop(0, TAPS // 8, tap_rows, 0)

    def tap_decay(g, carry):
        for jj in range(8):
            j = g * 8 + jj
            taps[rows(j, 1), :] = taps[rows(j, 1), :] * jnp.exp(-decb[...] * j.astype(F32))
        return carry

    lax.fori_loop(0, TAPS // 8, tap_decay, 0)

    queries_at = lax.broadcasted_iota(jnp.int32, (T, 2 * T), 0)
    keys_at = lax.broadcasted_iota(jnp.int32, (T, 2 * T), 1)
    low = lax.select(is_first, T, 0)
    seen = jnp.logical_and(keys_at <= queries_at + T, keys_at >= low)
    bias[...] = jnp.where(seen, 0.0, -1e30)

    def when_fed(value):
        pl.when(jnp.logical_not(is_first))(value)

    @pl.when(is_first)
    def _():
        rim_in[...] = jnp.zeros((160, HD), BF16)
        p_in[...] = jnp.zeros((TAPS * 8, HD), BF16)
        for h in range(HEADS):
            kcat[h, pl.ds(0, T), :] = jnp.zeros((T, HD), BF16)
            vcat[h, pl.ds(0, T), :] = jnp.zeros((T, HD), BF16)


    def se_block(i, carry):
        t = i * 8
        total = spread(ft[pl.ds(0, 8), :], 8) * se_p[rows(t + 8, 8), :]
        for j in range(1, LSE):
            total = total + spread(ft[pl.ds(j * 8, 8), :], 8) * se_p[rows(t + 8 - j, 8), :]
        se_mix[rows(t, 8), :] = total * feature(ut.at[0], wt, 0, t, 8)
        return carry

    lax.fori_loop(1, T // 8, se_block, 0)


    block = 16

    def tap_group(t, g, acc):
        j0 = g * 8
        acc = list(acc)
        window = [mr_p[rows(TAPS + t - j0 - 7 + s, 1), :] for s in range(block + 7)]
        for jj in range(8):
            tap = taps[rows(j0 + jj, 1), :]
            for s in range(block):
                acc[s] = acc[s] + tap * window[s + 7 - jj]
        return tuple(acc)

    def mr_own(i, carry):
        t = i * block
        zero = jnp.zeros((8, HD), F32)
        acc = lax.fori_loop(0, i * 2 - 1, lambda g, acc: tap_group(t, g, acc), (zero,) * block)
        for s in range(block):
            mr_mix[rows(t + s, 1), :] = acc[s]
        return carry

    for s in range(block):
        mr_mix[rows(s, 1), :] = jnp.zeros((8, HD), F32)
    lax.fori_loop(1, T // block, mr_own, 0)

    l_q.wait()
    sq[2] = jnp.zeros((T, HD), F32)

    def squares(mix, out_index):
        def step(i, carry):
            base = pl.multiple_of(i * 64, 64)
            total = jnp.zeros((8, HD), F32)
            for kk in range(8):
                x = mix[pl.ds(base + kk, 8, stride=8), :]
                total = total + x * x
            sq[out_index, pl.ds(pl.multiple_of(i * 8, 8), 8), :] = total
            return carry

        lax.fori_loop(0, T // 8, step, 0)

    ones = jnp.ones((8, HD), F32)

    def row_sums(index):
        return lax.dot_general(
            ones, sq[index], (((1,), (1,)), ((), ())),
            precision=HIGHEST, preferred_element_type=F32,
        )

    def st_copy(s, r):
        return pltpu.make_async_remote_copy(
            st_out.at[s], st_in.at[s, r - 1], st_send.at[s, r - 1], st_recv.at[s, r - 1],
            device_id=(c, lax.rem(p + r, n_panel)), device_id_type=MESH,
        )

    def share(s):
        for r in range(1, n_panel):
            st_copy(s, r).start()

    pick = (lax.broadcasted_iota(jnp.int32, (8, HD), 0) == 0).astype(F32)

    def scales(s, index):
        total = st_out[s, index, :, :T]
        for r in range(1, n_panel):
            total = total + st_in[s, r - 1, index, :, :T]
        scale = lax.rsqrt(total / CHANNELS + 1e-06)
        return lax.dot_general(
            scale, pick, (((0,), (0,)), ((), ())),
            precision=HIGHEST, preferred_element_type=F32,
        )

    def weigh(h):
        lanes = slice(h * HD, (h + 1) * HD)
        scores = lax.dot_general(
            qb[:, lanes], kcat[h], (((1,), (1,)), ((), ())), preferred_element_type=F32
        )
        scores = scores * (1.0 / math.sqrt(HD)) + bias[...]
        top = jnp.max(scores, axis=1, keepdims=True)
        raw = jnp.exp(scores - top)
        return raw.astype(BF16), jnp.sum(raw, axis=1, keepdims=True)

    def blend(h, raw, total):
        lanes = slice(h * HD, (h + 1) * HD)
        mixed = lax.dot_general(
            raw, vcat[h], (((1,), (0,)), ((), ())), preferred_element_type=F32
        )
        mixed = mixed * (1.0 / total)
        at_mix[:, lanes] = mixed
        return mixed * mixed

    def attend_pair(pair):
        when_fed(k_copy(pair).wait_recv)
        one, two = weigh(pair * 2), weigh(pair * 2 + 1)
        when_fed(v_copy(pair).wait_recv)
        sq[2] = sq[2] + (blend(pair * 2, *one) + blend(pair * 2 + 1, *two))

    attend_pair(0)


    when_fed(rim_copy.wait_recv)
    for i in range(6):
        ut[i, pl.ds(0, 16), :] = rim_in[pl.ds(64 + i * 16, 16), :].astype(F32)
    se_p[pl.ds(0, 64), :] = rim_in[pl.ds(0, 64), :].astype(F32)
    products(0, se_p, 8, 0, 2)
    products(1, mr_p, TAPS, 0, 2)
    se_block(0, 0)
    for part in range(QUARTERS):
        when_fed(p_copy(part).wait_recv)

    def prev_p(i, carry):
        mr_p[rows(i * 8, 8), :] = p_in[rows(i * 8, 8), :].astype(F32)
        return carry

    lax.fori_loop(0, TAPS // 8, prev_p, 0)

    def mr_rest(i, carry):
        t = i * block
        acc = tuple(mr_mix[rows(t + s, 1), :] for s in range(block))
        start = lax.max(i * 2 - 1, 0)
        acc = lax.fori_loop(start, TAPS // 8, lambda g, acc: tap_group(t, g, acc), acc)
        gate = feature(ut.at[3], wt, 9, t, block)
        for s in range(block):
            mr_mix[rows(t + s, 1), :] = acc[s] * gate[s * 8 : s * 8 + 8]

        return carry

    lax.fori_loop(0, T // block, mr_rest, 0)

    attend_pair(1)

    squares(se_mix, 0)
    squares(mr_mix, 1)
    st_out[0, 0, :, :T] = row_sums(0)
    st_out[0, 1, :, :T] = row_sums(1)
    share(0)

    attend_pair(2)

    for r in range(1, n_panel):
        st_copy(0, r).wait_recv()
    for index, mix, out in ((0, se_mix, se_out), (1, mr_mix, mr_out)):
        sq[index] = scales(0, index)

        def finish(i, carry):
            r = pl.multiple_of(i * 16, 16)
            for kk in range(8):
                parts = []
                for hh in range(2):
                    x = mix[pl.ds((r + hh * 8) * 8 + kk, 8, stride=8), :]
                    parts.append(x * sq[index, pl.ds(r + hh * 8, 8), :])
                out[pl.ds(r, 16), kk * HD : (kk + 1) * HD] = jnp.concatenate(parts, 0).astype(BF16)
            return carry

        lax.fori_loop(0, T // 16, finish, 0)

    attend_pair(3)

    st_out[1, 0, :, :T] = row_sums(2)
    share(1)
    for r in range(1, n_panel):
        st_copy(1, r).wait_recv()
    sq[2] = scales(1, 0)
    for h in range(HEADS):
        at_out[:, h * HD : (h + 1) * HD] = (at_mix[:, h * HD : (h + 1) * HD] * sq[2]).astype(BF16)

    for s in range(2):
        for r in range(1, n_panel):
            st_copy(s, r).wait_send()

    @pl.when(has_dst)
    def _():
        rim_copy.wait_send()
        for part in range(QUARTERS):
            p_copy(part).wait_send()
        for pair in range(PAIRS):
            k_copy(pair).wait_send()
            v_copy(pair).wait_send()


def writer(a, b, c, x, y, z, sems):
    copies = [
        pltpu.make_async_copy(i, o, sems.at[n]) for n, (i, o) in enumerate(((a, x), (b, y), (c, z)))
    ]
    for copy in copies:
        copy.start()
    for copy in copies:
        copy.wait()


def body(n_ctx, n_panel, se_u, se_w, se_f, mr_u, mr_w, mr_raw, mr_decay, q, k, v):
    anywhere = pl.BlockSpec(memory_space=pl.ANY)
    vmem = pl.BlockSpec(memory_space=pltpu.VMEM)
    out = pltpu.VMEM((T, WIDTH), BF16)
    plain = jax.ShapeDtypeStruct((T, WIDTH), BF16)
    dma = pltpu.SemaphoreType.DMA
    mixed = pl.pallas_call(
        functools.partial(kernel, n_ctx, n_panel),
        out_shape=(out, out, out),
        in_specs=[anywhere] * 10,
        out_specs=(vmem, vmem, vmem),
        scratch_shapes=[
            pltpu.VMEM((6, T, WIDTH), BF16),
            pltpu.VMEM((2, 3, 3, WIDTH), F32),
            pltpu.VMEM((LSE, WIDTH), F32),
            pltpu.VMEM((TAPS, WIDTH), F32),
            pltpu.VMEM((8, HD), F32),
            pltpu.VMEM((T, WIDTH), BF16),
            pltpu.VMEM((HEADS, 2 * T, HD), BF16),
            pltpu.VMEM((HEADS, 2 * T, HD), BF16),
            pltpu.VMEM((6, (T + 2) * 8, HD), F32),
            pltpu.VMEM((18 * 8, HD), F32),
            pltpu.VMEM((8 * 8, HD), F32),
            pltpu.VMEM((TAPS * 8, HD), F32),
            pltpu.VMEM(((T + 8) * 8, HD), F32),
            pltpu.VMEM(((T + TAPS) * 8, HD), F32),
            pltpu.VMEM((T * 8, HD), F32),
            pltpu.VMEM((T * 8, HD), F32),
            pltpu.VMEM((T, WIDTH), F32),
            pltpu.VMEM((T, 2 * T), F32),
            pltpu.VMEM((3, T, HD), F32),
            pltpu.VMEM((160, HD), BF16),
            pltpu.VMEM((160, HD), BF16),
            pltpu.VMEM((TAPS * 8, HD), BF16),
            pltpu.VMEM((TAPS * 8, HD), BF16),
            pltpu.VMEM((2, 2, 8, 256), F32),
            pltpu.VMEM((2, n_panel - 1, 2, 8, 256), F32),
            dma((12 + 2 * HEADS,)),
            dma((2,)),
            dma((QUARTERS,)),
            dma((QUARTERS,)),
            dma((PAIRS,)),
            dma((PAIRS,)),
            dma((PAIRS,)),
            dma((PAIRS,)),
            dma((2, n_panel - 1)),
            dma((2, n_panel - 1)),
        ],
        compiler_params=pltpu.CompilerParams(collective_id=0, has_side_effects=True),
        name="mixer",
    )(se_u, se_w, se_f, mr_u, mr_w, mr_raw, mr_decay.reshape(8, HD), q, k, v)
    return pl.pallas_call(
        writer,
        out_shape=(plain, plain, plain),
        in_specs=[vmem] * 3,
        out_specs=[anywhere] * 3,
        scratch_shapes=[dma((3,))],
        name="writer",
    )(*(pltpu.with_memory_space_constraint(x, pltpu.VMEM) for x in mixed))


def solution(mesh):
    placed = (
        P(None, "ctx", "panel"),
        P(None, None, "panel"),
        P(None, "panel"),
        P(None, "ctx", "panel"),
        P(None, None, "panel"),
        P(None, "panel"),
        P("panel"),
        P("ctx", "panel"),
        P("ctx", "panel"),
        P("ctx", "panel"),
    )
    return jax.shard_map(
        functools.partial(body, mesh.shape["ctx"], mesh.shape["panel"]),
        mesh=mesh,
        in_specs=placed,
        out_specs=(P("ctx", "panel"), P("ctx", "panel"), P("ctx", "panel")),
        check_vma=False,
    )
```
